32 devices in a mesh: grp: 2 (over y), ep: 4 (over z), dp: 4 (over x, core).
Axes of the slice: x: 2, y: 2, z: 4, core: 2. Of those that a mesh axis runs over, the one named last changes fastest.
Arguments:
- tokens: bfloat16 [128, 7168], P(('grp', 'ep', 'dp')), parts along dimension 0, may hold values from -6 to 6
- expert_ids: int32 [128, 8], P(('grp', 'ep', 'dp')), parts along dimension 0, may hold values from 0 to 15, all different within a row; in each aligned block of 4 rows (0 to 3, 4 to 7, ...) at most 3 rows name the same one
- combine_weight: float32 [128, 8], P(('grp', 'ep', 'dp')), parts along dimension 0, may hold values from 0.1 to 1
- slot_of_expert: int32 [16], replicated, may hold values from 0 to 15, each once
- w_gate: bfloat16 [16, 7168, 2048], P('ep', None, 'dp'), may hold values from -0.0625 to 0.0625
- w_up: bfloat16 [16, 7168, 2048], P('ep', None, 'dp'), may hold values from -0.0625 to 0.0625
- w_down: bfloat16 [16, 2048, 7168], P('ep', 'dp'), may hold values from -0.125 to 0.125
Outputs:
- mixed: bfloat16 [128, 7168], P(('grp', 'ep', 'dp')), parts along dimension 0
The draws below stay inside these ranges and needn't reach their ends.
There are 2 independent parts, one for each index of `grp`. The reference program is written for one: setup_inputs(seed, part) draws one part's arguments, and reference() takes and returns one part's arrays. A program takes and returns all parts, laid end to end along the dimension named above; an argument that names none is the same for every part. Nothing has to cross between parts.
Inputs may be any that keep to these rules, and one draw needn't show every extreme that they name: `expert_ids`: among the rows of one device no expert is named by more than 3 rows. `slot_of_expert`: every stored slot serves exactly one expert.
All inputs are finite; a program needn't handle non-finite values.
Results may differ from the reference program's by a relative error of at most 0.015.
Values may be sent and summed in bfloat16 or wider, within the bound.
No kernel may reach another device: no remote copies, remote signals or barrier semaphores. Data moves between devices by JAX's collectives and lax.ppermute only.
A program may use at most 128 MiB of HBM per device.

```python
import math
import jax
import jax.numpy as jnp
import numpy as np
from jax import lax

D = 7168
FF = 2048
TOP = 8
EXPERTS = 16
T_DEV = 4
CAP = 3
TOKENS = 64
N_DP = 4


def levels(key, extent, cuts, low, largest):
    def one(position, shards_of):
        heights = jax.random.uniform(jax.random.fold_in(jax.random.fold_in(key, 6), position), (shards_of,), jnp.float32, low / len(cuts), largest / len(cuts))
        return jnp.repeat(jnp.exp(heights), extent[position] // shards_of).reshape((-1,) + (1,) * (len(extent) - position - 1))

    loudness = one(*cuts[0])
    for cut in cuts[1:]:
        loudness = loudness * one(*cut)
    return loudness


def assign_block(key, own, number, rows, number_of, top, reach, skew):
    sequence = jax.random.permutation(key, number_of)
    crowded, ordinary = portions_of(number_of, rows * top, reach, skew, True), portions_of(number_of, rows * top, reach, skew, False)
    places = jnp.arange(number_of)

    def named(lengths, rotation):
        used = int((lengths > 0).sum())
        fixed = max(1, used // 4)
        moved = fixed + (places - fixed + rotation * (used - fixed)) % max(1, number_of - fixed)
        return jnp.zeros((number_of,), jnp.int32).at[sequence[jnp.where(places < fixed, places, moved)]].set(jnp.asarray(lengths, jnp.int32))

    lengths = jnp.where(number % 4 == 0, named(crowded, number // 4), named(ordinary, number - number // 4 - 1))
    mixed = jax.random.permutation(jax.random.fold_in(own, 3), number_of)
    giver, sink = mixed[0:number_of // 2 * 2:2], mixed[1:number_of // 2 * 2:2]
    slack = jnp.minimum(lengths[giver] - 1, reach - lengths[sink]) // 2
    slack = jnp.where((giver == sequence[0]) | (sink == sequence[0]) | (lengths[sink] == 0), 0, jnp.maximum(slack, 0))
    moved = jax.random.randint(jax.random.fold_in(own, 4), (number_of // 2,), 0, 1 << 20) % (slack + 1)
    lengths = lengths.at[giver].add(-moved).at[sink].add(moved)
    labels = jnp.searchsorted(jnp.cumsum(lengths), jnp.arange(rows * top), side="right").astype(jnp.int32)
    listing = labels.reshape(top, rows).T
    listing = listing[jax.random.permutation(jax.random.fold_in(own, 1), rows)]
    rotation = jax.random.randint(jax.random.fold_in(own, 2), (rows, 1), 0, top)
    return jnp.take_along_axis(listing, (jnp.arange(top)[None, :] + rotation) % top, axis=1)


def portions_of(count, total, bound, skew, full):
    loads = [(1 << 20) // math.isqrt(rank ** skew) + 1 for rank in range(1, count + 1)]
    largest = bound if full else min(bound, max(-(-total // count), total * loads[0] // sum(loads)))
    least = 1 if total - largest >= count - 1 else 0
    holding, spare = [largest] + [least] * (count - 1), total - largest - least * (count - 1)
    while spare > 0:
        free = [i for i in range(1, count) if holding[i] < largest] or [i for i in range(1, count) if holding[i] < bound]
        mass, budget = sum([loads[i] for i in free]), spare
        for i in free:
            addition = min(bound - holding[i], max(1, budget * loads[i] // mass), spare)
            holding[i] = holding[i] + addition
            spare = spare - addition
    return np.array(holding)


def bell_draw(key, dims, deviation, limit, pieces=(), held_as=jnp.bfloat16):
    values = deviation * jax.random.normal(key, dims, jnp.float32)
    if pieces:
        values = values * levels(key, dims, pieces, -0.22, 0.18)
    return jnp.clip(values, -limit, limit).astype(held_as)


def setup_inputs(seed: int = 0, part: int = 0) -> dict:
    arg_keys = jax.random.split(jax.random.key(seed), 8)
    own_keys = jax.random.split(jax.random.fold_in(arg_keys[7], part), 8)
    tokens = bell_draw(own_keys[0], (TOKENS, D), 1.0, 6.0, ((0, 16),))
    expert_ids_keys = jax.random.split(jax.random.fold_in(own_keys[1], 1), TOKENS // T_DEV)
    expert_ids_turns = jax.random.permutation(jax.random.fold_in(own_keys[1], 3), TOKENS // T_DEV)
    expert_ids = jax.vmap(lambda own, number: assign_block(jax.random.fold_in(own_keys[1], 2), own, number, T_DEV, EXPERTS, TOP, CAP, 2))(expert_ids_keys, expert_ids_turns).reshape((TOKENS, TOP))
    combine_weight = jnp.clip(jnp.exp(math.log(1.0) - 2.3025851 * jax.random.uniform(own_keys[2], (TOKENS, TOP), jnp.float32) ** levels(own_keys[2], (TOKENS, TOP), ((0, 16),), -0.2, 0.2)), 0.1, 1.0)
    slot_of_expert = jax.random.permutation(arg_keys[3], EXPERTS).astype(jnp.int32)
    w_gate = bell_draw(arg_keys[4], (EXPERTS, D, FF), D ** -0.5, 0.0625, ((0, 4), (2, 4)))
    w_up = bell_draw(arg_keys[5], (EXPERTS, D, FF), D ** -0.5, 0.0625, ((0, 4), (2, 4)))
    w_down = bell_draw(arg_keys[6], (EXPERTS, FF, D), FF ** -0.5, 0.125, ((0, 4), (1, 4)))
    return dict(tokens=tokens, expert_ids=expert_ids, combine_weight=combine_weight, slot_of_expert=slot_of_expert, w_gate=w_gate, w_up=w_up, w_down=w_down)


def round_trip(values):
    return lax.optimization_barrier(values.astype(jnp.bfloat16)).astype(jnp.float32)


def reference(tokens, expert_ids, combine_weight, slot_of_expert, w_gate, w_up, w_down):
    rows = tokens.astype(jnp.float32)
    count = rows.shape[0]
    group = FF // N_DP
    slots = slot_of_expert[expert_ids]

    def add_slot(index, total):
        gate = jnp.dot(rows, w_gate[index].astype(jnp.float32), precision=lax.Precision.HIGHEST)
        upper = jnp.dot(rows, w_up[index].astype(jnp.float32), precision=lax.Precision.HIGHEST)
        hidden = round_trip(jax.nn.silu(gate) * upper)
        down = w_down[index].astype(jnp.float32).reshape(N_DP, group, D)
        parts = jnp.einsum("tqf,qfd->tqd", hidden.reshape(count, N_DP, group), down, precision=lax.Precision.HIGHEST)
        expert_out = round_trip(jnp.sum(round_trip(parts), axis=1))
        weight = jnp.sum(jnp.where(slots == index, combine_weight, jnp.float32(0.0)), axis=1)
        return total + weight[:, None] * expert_out

    total = lax.fori_loop(0, EXPERTS, add_slot, jnp.zeros((count, D), jnp.float32))
    return total.astype(jnp.bfloat16)
```

```python
import functools

import jax
import jax.numpy as jnp
from jax import lax
from jax.experimental import pallas as pl
from jax.experimental.pallas import tpu as pltpu
from jax.sharding import PartitionSpec as P

LANES = 128
MIB = 1 << 20
VMEM = pl.BlockSpec(memory_space=pltpu.VMEM)
SMEM = pl.BlockSpec(memory_space=pltpu.SMEM)
ANY = pl.BlockSpec(memory_space=pl.ANY)


def pack_kernel(slot_ref, tokens_ref, ids_ref, weight_ref, out_ref):
    rows, width = tokens_ref.shape
    experts = slot_ref.shape[0]
    extra = out_ref.shape[1] - width
    lane = lax.broadcasted_iota(jnp.int32, (rows, extra), 1)
    ids = ids_ref[...]
    weight = weight_ref[...]
    by_slot = jnp.zeros((rows, extra), jnp.float32)
    slot = jnp.zeros(ids.shape, jnp.int32)
    for e in range(experts):
        slot = jnp.where(ids == e, slot_ref[e], slot)
    for k in range(ids.shape[1]):
        by_slot = by_slot + jnp.where(lane == slot[:, k : k + 1], weight[:, k : k + 1], 0.0)
    high = by_slot.astype(jnp.bfloat16)
    low = by_slot - high.astype(jnp.float32)
    low = pltpu.roll(low, experts, 1)
    columns = jnp.where(lane < experts, high.astype(jnp.float32), low)
    out_ref[:, :width] = tokens_ref[...]
    out_ref[:, width:] = columns.astype(jnp.bfloat16)


def hidden_kernel(units, width, parts, ahead, *refs):
    pieces = refs[:units]
    gate_ref, up_ref, down_ref, hidden_ref, early_ref = refs[units : units + 5]
    x_ref, coef_ref, ring_ref, up_sem, down_sem = refs[units + 5 :]
    slots, _, ff = gate_ref.shape
    experts = coef_ref.shape[2]
    depth = width // parts
    slots_ring = ring_ref.shape[0]
    chunk = early_ref.shape[3]

    def up_copy(step):
        j, p = step // parts, step % parts
        place = lax.rem(step, slots_ring)
        return pltpu.make_async_copy(
            up_ref.at[j, pl.ds(pl.multiple_of(p * depth, depth), depth)], ring_ref.at[place], up_sem.at[place]
        )

    def down_copy(c, j):
        return pltpu.make_async_copy(
            down_ref.at[j, :, pl.ds(c * chunk, chunk)], early_ref.at[c, j], down_sem.at[c, j]
        )

    for step in range(min(slots_ring, slots * parts)):
        up_copy(step).start()
    row = 0
    for piece in pieces:
        count = piece.shape[0]
        x_ref[row : row + count, :] = piece[:, :width]
        coef_ref[0, row : row + count, :] = piece[:, width : width + experts].astype(jnp.float32)
        coef_ref[1, row : row + count, :] = piece[:, width + experts : width + 2 * experts].astype(jnp.float32)
        row += count
    lane = lax.broadcasted_iota(jnp.int32, coef_ref.shape[1:], 1)

    def one(j, carry):
        for c in range(ahead):
            down_copy(c, j).start()
        gate = jnp.dot(x_ref[...], gate_ref[j], preferred_element_type=jnp.float32)
        upper = jnp.zeros(gate.shape, jnp.float32)
        for p in range(parts):
            step = j * parts + p
            up_copy(step).wait()
            upper = upper + jnp.dot(
                x_ref[:, p * depth : (p + 1) * depth],
                ring_ref[lax.rem(step, slots_ring)],
                preferred_element_type=jnp.float32,
            )

            @pl.when(step + slots_ring < slots * parts)
            def _():
                up_copy(step + slots_ring).start()

        own = lane == lax.axis_index("ep") * slots + j
        coef = jnp.sum(jnp.where(own, coef_ref[0] + coef_ref[1], 0.0), axis=1, keepdims=True)
        hidden = gate / (1.0 + jnp.exp(-gate)) * upper * coef
        hidden_ref[:, pl.ds(pl.multiple_of(j * ff, ff), ff)] = hidden.astype(jnp.bfloat16)
        return carry

    lax.fori_loop(0, slots, one, 0)
    for c in range(ahead):
        for j in range(slots):
            down_copy(c, j).wait()


def down_kernel(units, ahead, hidden_ref, early_ref, down_ref, *refs):
    outs = refs[:units]
    late_ref, sem = refs[units:]
    slots, ff, width = down_ref.shape
    chunk = early_ref.shape[3]
    late = late_ref.shape[0]

    def copy(c, j):
        return pltpu.make_async_copy(
            down_ref.at[j, :, pl.ds((ahead + c) * chunk, chunk)], late_ref.at[c, j], sem.at[c, j]
        )

    for c in range(late):
        for j in range(slots):
            copy(c, j).start()
    hidden = hidden_ref[...]
    for c in range(ahead + late):
        if c >= ahead:
            for j in range(slots):
                copy(c - ahead, j).wait()
        block = early_ref[c] if c < ahead else late_ref[c - ahead]
        total = jnp.dot(hidden, block.reshape(slots * ff, chunk), preferred_element_type=jnp.float32)
        total = total.astype(jnp.bfloat16)
        row = 0
        for out in outs:
            count = out.shape[0]
            out[:, c * chunk : (c + 1) * chunk] = total[row : row + count]
            row += count


def add(*terms):
    total = terms[0].astype(jnp.float32)
    for term in terms[1:]:
        total = total + term.astype(jnp.float32)
    return total.astype(jnp.bfloat16)


def toward(size, shift):
    return [(i, (i + shift) % size) for i in range(size)]


def body(tokens, expert_ids, combine_weight, slot_of_expert, w_gate, w_up, w_down):
    ep, dp = lax.axis_size("ep"), lax.axis_size("dp")
    core = 2 if dp % 2 == 0 else 1
    chips = dp // core
    rows, width = tokens.shape
    slots, _, ff = w_gate.shape
    experts = slot_of_expert.shape[0]
    extra = -(-2 * experts // LANES) * LANES
    total_rows = rows * ep * dp
    groups = min(ep, 4)

    def step_z(value, shift):
        return lax.ppermute(value, "ep", toward(ep, shift))

    def step_x(value, shift):
        return lax.ppermute(value, "dp", toward(dp, shift * core))

    def step_core(value):
        return lax.ppermute(value, "dp", [(i, i ^ 1) for i in range(dp)])

    packed = pl.pallas_call(
        pack_kernel,
        out_shape=jax.ShapeDtypeStruct((rows, width + extra), jnp.bfloat16),
        in_specs=[SMEM, VMEM, VMEM, VMEM],
        out_specs=VMEM,
        cost_estimate=pl.CostEstimate(flops=0, bytes_accessed=64 * MIB, transcendentals=0),
        compiler_params=pltpu.CompilerParams(vmem_limit_bytes=2 * MIB),
        name="pack",
    )(slot_of_expert, tokens, expert_ids, combine_weight)

    along_z = [packed] + [step_z(packed, -s) for s in range(1, ep)]
    per = ep // groups
    along_z = [
        along_z[g * per] if per == 1 else jnp.concatenate(along_z[g * per : (g + 1) * per], axis=0)
        for g in range(groups)
    ]
    units = list(along_z)
    for s in range(1, chips):
        units += [step_x(unit, -s) for unit in along_z]
    if core == 2:
        units += [step_core(unit) for unit in units]
    count = len(units)
    unit_rows = units[0].shape[0]

    chunk = next(c for c in (1024, 512, 256, 128, width) if width % c == 0)
    chunks = width // chunk
    ahead = max(1, chunks * 2 // 7)
    parts = 2 if width % 256 == 0 else 1
    ring = min(4, slots * parts)
    gate_in = pltpu.with_memory_space_constraint(w_gate, pltpu.VMEM)
    hidden, early = pl.pallas_call(
        functools.partial(hidden_kernel, count, width, parts, ahead),
        out_shape=(
            pltpu.VMEM((total_rows, slots * ff), jnp.bfloat16),
            pltpu.VMEM((ahead, slots, ff, chunk), jnp.bfloat16),
        ),
        in_specs=[VMEM] * (count + 1) + [ANY, ANY],
        out_specs=(VMEM, VMEM),
        scratch_shapes=[
            pltpu.VMEM((total_rows, width), jnp.bfloat16),
            pltpu.VMEM((2, total_rows, experts), jnp.float32),
            pltpu.VMEM((ring, width // parts, ff), jnp.bfloat16),
            pltpu.SemaphoreType.DMA((ring,)),
            pltpu.SemaphoreType.DMA((ahead, slots)),
        ],
        cost_estimate=pl.CostEstimate(
            flops=4 * total_rows * slots * ff * width,
            bytes_accessed=6 * slots * ff * width,
            transcendentals=total_rows * slots * ff,
        ),
        compiler_params=pltpu.CompilerParams(vmem_limit_bytes=21 * MIB),
        name="hidden",
    )(*units, gate_in, w_up, w_down)

    outs = pl.pallas_call(
        functools.partial(down_kernel, count, ahead),
        out_shape=[jax.ShapeDtypeStruct((unit_rows, width), jnp.bfloat16)] * count,
        in_specs=[VMEM, VMEM, ANY],
        out_specs=[VMEM] * count,
        scratch_shapes=[
            pltpu.VMEM((chunks - ahead, slots, ff, chunk), jnp.bfloat16),
            pltpu.SemaphoreType.DMA((chunks - ahead, slots)),
        ],
        cost_estimate=pl.CostEstimate(
            flops=2 * total_rows * slots * ff * width, bytes_accessed=2 * slots * ff * width, transcendentals=0
        ),
        compiler_params=pltpu.CompilerParams(vmem_limit_bytes=40 * MIB),
        name="down",
    )(hidden, early, w_down)

    outs = [[value] for value in outs]
    if core == 2:
        half = count // 2
        moved = [None] * half
        for u in list(range(groups, half)) + list(range(groups)):
            moved[u] = step_core(outs[half + u][0])
        for u in range(half):
            outs[u].append(moved[u])
        outs = outs[:half]
    for s in range(1, chips):
        for g in range(groups):
            outs[g].append(step_x(add(*outs[s * groups + g]), s))
    held = []
    for g in range(groups):
        for i in range(per):
            held.append([term[i * rows : (i + 1) * rows] for term in outs[g]])
    final = held[0]
    for s in range(1, ep):
        final.append(step_z(add(*held[s]), s))
    return add(*final)


def solution(mesh):
    in_specs = (
        P(("grp", "ep", "dp"), None),
        P(("grp", "ep", "dp"), None),
        P(("grp", "ep", "dp"), None),
        P(),
        P("ep", None, "dp"),
        P("ep", None, "dp"),
        P("ep", "dp", None),
    )
    out_specs = P(("grp", "ep", "dp"), None)
    return jax.shard_map(body, mesh=mesh, in_specs=in_specs, out_specs=out_specs, check_vma=False)
```

```python
import functools

import jax
import jax.numpy as jnp
from jax import lax
from jax.experimental import pallas as pl
from jax.experimental.pallas import tpu as pltpu
from jax.sharding import PartitionSpec as P

LANES = 128
MIB = 1 << 20
VMEM = pl.BlockSpec(memory_space=pltpu.VMEM)
HBM = pl.BlockSpec(memory_space=pltpu.HBM)


def pack_kernel(slot_hbm, tokens_hbm, ids_hbm, weight_hbm, out_ref, slot_ref, ids_ref, weight_ref, sem):
    rows, width = tokens_hbm.shape
    copies = [
        pltpu.make_async_copy(slot_hbm, slot_ref, sem.at[0]),
        pltpu.make_async_copy(ids_hbm, ids_ref, sem.at[1]),
        pltpu.make_async_copy(weight_hbm, weight_ref, sem.at[2]),
        pltpu.make_async_copy(tokens_hbm, out_ref.at[:, pl.ds(0, width)], sem.at[3]),
    ]
    for copy in copies:
        copy.start()
    for copy in copies:
        copy.wait()
    experts = slot_ref.shape[0]
    extra = out_ref.shape[1] - width
    lane = lax.broadcasted_iota(jnp.int32, (rows, extra), 1)
    ids = ids_ref[...]
    weight = weight_ref[...]
    by_slot = jnp.zeros((rows, extra), jnp.float32)
    slot = jnp.zeros(ids.shape, jnp.int32)
    for e in range(experts):
        slot = jnp.where(ids == e, slot_ref[e], slot)
    for k in range(ids.shape[1]):
        by_slot = by_slot + jnp.where(lane == slot[:, k : k + 1], weight[:, k : k + 1], 0.0)
    high = by_slot.astype(jnp.bfloat16)
    low = by_slot - high.astype(jnp.float32)
    low = pltpu.roll(low, experts, 1)
    columns = jnp.where(lane < experts, high.astype(jnp.float32), low)
    out_ref[:, width:] = columns.astype(jnp.bfloat16)


def hidden_kernel(units, width, parts, ahead, *refs):
    pieces = refs[:units]
    gate_ref, up_ref, down_ref, hidden_ref, early_ref = refs[units : units + 5]
    x_ref, coef_ref, ring_ref, up_sem, down_sem = refs[units + 5 :]
    slots, _, ff = gate_ref.shape
    experts = coef_ref.shape[2]
    depth = width // parts
    slots_ring = ring_ref.shape[0]
    chunk = early_ref.shape[3]

    def up_copy(step):
        j, p = step // parts, step % parts
        place = lax.rem(step, slots_ring)
        return pltpu.make_async_copy(
            up_ref.at[j, pl.ds(pl.multiple_of(p * depth, depth), depth)], ring_ref.at[place], up_sem.at[place]
        )

    def down_copy(c, j):
        return pltpu.make_async_copy(
            down_ref.at[j, :, pl.ds(c * chunk, chunk)], early_ref.at[c, j], down_sem.at[c, j]
        )

    for step in range(min(slots_ring, slots * parts)):
        up_copy(step).start()
    row = 0
    for piece in pieces:
        count = piece.shape[0]
        x_ref[row : row + count, :] = piece[:, :width]
        coef_ref[0, row : row + count, :] = piece[:, width : width + experts].astype(jnp.float32)
        coef_ref[1, row : row + count, :] = piece[:, width + experts : width + 2 * experts].astype(jnp.float32)
        row += count
    lane = lax.broadcasted_iota(jnp.int32, coef_ref.shape[1:], 1)

    def one(j, carry):
        for c in range(ahead):
            down_copy(c, j).start()
        gate = jnp.dot(x_ref[...], gate_ref[j], preferred_element_type=jnp.float32)
        upper = jnp.zeros(gate.shape, jnp.float32)
        for p in range(parts):
            step = j * parts + p
            up_copy(step).wait()
            upper = upper + jnp.dot(
                x_ref[:, p * depth : (p + 1) * depth],
                ring_ref[lax.rem(step, slots_ring)],
                preferred_element_type=jnp.float32,
            )

            @pl.when(step + slots_ring < slots * parts)
            def _():
                up_copy(step + slots_ring).start()

        own = lane == lax.axis_index("ep") * slots + j
        coef = jnp.sum(jnp.where(own, coef_ref[0] + coef_ref[1], 0.0), axis=1, keepdims=True)
        hidden = gate / (1.0 + jnp.exp(-gate)) * upper * coef
        hidden_ref[:, pl.ds(pl.multiple_of(j * ff, ff), ff)] = hidden.astype(jnp.bfloat16)
        return carry

    lax.fori_loop(0, slots, one, 0)
    for c in range(ahead):
        for j in range(slots):
            down_copy(c, j).wait()


def down_kernel(units, ahead, hidden_ref, early_ref, down_ref, *refs):
    outs = refs[:units]
    late_ref, sem = refs[units:]
    slots, ff, width = down_ref.shape
    chunk = early_ref.shape[3]
    late = late_ref.shape[0]

    def copy(c, j):
        return pltpu.make_async_copy(
            down_ref.at[j, :, pl.ds((ahead + c) * chunk, chunk)], late_ref.at[c, j], sem.at[c, j]
        )

    for c in range(late):
        for j in range(slots):
            copy(c, j).start()
    hidden = hidden_ref[...]
    for c in range(ahead + late):
        if c >= ahead:
            for j in range(slots):
                copy(c - ahead, j).wait()
        block = early_ref[c] if c < ahead else late_ref[c - ahead]
        total = jnp.dot(hidden, block.reshape(slots * ff, chunk), preferred_element_type=jnp.float32)
        total = total.astype(jnp.bfloat16)
        row = 0
        for out in outs:
            count = out.shape[0]
            out[:, c * chunk : (c + 1) * chunk] = total[row : row + count]
            row += count


def add(*terms):
    total = terms[0].astype(jnp.float32)
    for term in terms[1:]:
        total = total + term.astype(jnp.float32)
    return total.astype(jnp.bfloat16)


def toward(size, shift):
    return [(i, (i + shift) % size) for i in range(size)]


def body(tokens, expert_ids, combine_weight, slot_of_expert, w_gate, w_up, w_down):
    ep, dp = lax.axis_size("ep"), lax.axis_size("dp")
    core = 2 if dp % 2 == 0 else 1
    chips = dp // core
    rows, width = tokens.shape
    slots, _, ff = w_gate.shape
    experts = slot_of_expert.shape[0]
    extra = -(-2 * experts // LANES) * LANES
    total_rows = rows * ep * dp
    groups = min(ep, 4)

    def step_z(value, shift):
        return lax.ppermute(value, "ep", toward(ep, shift))

    def step_x(value, shift):
        return lax.ppermute(value, "dp", toward(dp, shift * core))

    def step_core(value):
        return lax.ppermute(value, "dp", [(i, i ^ 1) for i in range(dp)])

    packed = pl.pallas_call(
        pack_kernel,
        out_shape=jax.ShapeDtypeStruct((rows, width + extra), jnp.bfloat16),
        in_specs=[HBM] * 4,
        out_specs=VMEM,
        scratch_shapes=[
            pltpu.SMEM(slot_of_expert.shape, jnp.int32),
            pltpu.VMEM(expert_ids.shape, jnp.int32),
            pltpu.VMEM(combine_weight.shape, jnp.float32),
            pltpu.SemaphoreType.DMA((4,)),
        ],
        cost_estimate=pl.CostEstimate(flops=30 * slots * ff * width * 64, bytes_accessed=64 * MIB, transcendentals=0),
        compiler_params=pltpu.CompilerParams(vmem_limit_bytes=2 * MIB),
        name="pack",
    )(*[pltpu.with_memory_space_constraint(value, pltpu.HBM) for value in (slot_of_expert, tokens, expert_ids, combine_weight)])

    along_z = [packed] + [step_z(packed, -s) for s in range(1, ep)]
    per = ep // groups
    along_z = [
        along_z[g * per] if per == 1 else jnp.concatenate(along_z[g * per : (g + 1) * per], axis=0)
        for g in range(groups)
    ]
    units = list(along_z)
    for s in range(1, chips):
        units += [step_x(unit, -s) for unit in along_z]
    if core == 2:
        units += [step_core(unit) for unit in units]
    count = len(units)
    unit_rows = units[0].shape[0]

    chunk = next(c for c in (1024, 512, 256, 128, width) if width % c == 0)
    chunks = width // chunk
    ahead = max(1, chunks * 2 // 7)
    parts = 2 if width % 256 == 0 else 1
    ring = min(4, slots * parts)
    gate_in, *held = [pltpu.with_memory_space_constraint(value, pltpu.VMEM) for value in (w_gate, *units)]
    hidden, early = pl.pallas_call(
        functools.partial(hidden_kernel, count, width, parts, ahead),
        out_shape=(
            pltpu.VMEM((total_rows, slots * ff), jnp.bfloat16),
            pltpu.VMEM((ahead, slots, ff, chunk), jnp.bfloat16),
        ),
        in_specs=[VMEM] * (count + 1) + [HBM, HBM],
        out_specs=(VMEM, VMEM),
        scratch_shapes=[
            pltpu.VMEM((total_rows, width), jnp.bfloat16),
            pltpu.VMEM((2, total_rows, experts), jnp.float32),
            pltpu.VMEM((ring, width // parts, ff), jnp.bfloat16),
            pltpu.SemaphoreType.DMA((ring,)),
            pltpu.SemaphoreType.DMA((ahead, slots)),
        ],
        cost_estimate=pl.CostEstimate(
            flops=4 * total_rows * slots * ff * width,
            bytes_accessed=6 * slots * ff * width,
            transcendentals=total_rows * slots * ff,
        ),
        compiler_params=pltpu.CompilerParams(vmem_limit_bytes=21 * MIB),
        name="hidden",
    )(*held, gate_in, w_up, w_down)

    outs = pl.pallas_call(
        functools.partial(down_kernel, count, ahead),
        out_shape=[jax.ShapeDtypeStruct((unit_rows, width), jnp.bfloat16)] * count,
        in_specs=[VMEM, VMEM, HBM],
        out_specs=[VMEM] * count,
        scratch_shapes=[
            pltpu.VMEM((chunks - ahead, slots, ff, chunk), jnp.bfloat16),
            pltpu.SemaphoreType.DMA((chunks - ahead, slots)),
        ],
        cost_estimate=pl.CostEstimate(
            flops=2 * total_rows * slots * ff * width, bytes_accessed=2 * slots * ff * width, transcendentals=0
        ),
        compiler_params=pltpu.CompilerParams(vmem_limit_bytes=40 * MIB),
        name="down",
    )(hidden, early, w_down)

    outs = [[value] for value in outs]
    if core == 2:
        half = count // 2
        moved = [None] * half
        for u in list(range(groups, half)) + list(range(groups)):
            moved[u] = step_core(outs[half + u][0])
        for u in range(half):
            outs[u].append(moved[u])
        outs = outs[:half]
    for s in range(1, chips):
        for g in range(groups):
            outs[g].append(step_x(add(*outs[s * groups + g]), s))
    held = []
    for g in range(groups):
        for i in range(per):
            held.append([term[i * rows : (i + 1) * rows] for term in outs[g]])
    final = held[0]
    for s in range(1, ep):
        final.append(step_z(add(*held[s]), s))
    return add(*final)


def solution(mesh):
    in_specs = (
        P(("grp", "ep", "dp"), None),
        P(("grp", "ep", "dp"), None),
        P(("grp", "ep", "dp"), None),
        P(),
        P("ep", None, "dp"),
        P("ep", None, "dp"),
        P("ep", "dp", None),
    )
    out_specs = P(("grp", "ep", "dp"), None)
    return jax.shard_map(body, mesh=mesh, in_specs=in_specs, out_specs=out_specs, check_vma=False)
```

```python
import functools

import jax
import jax.numpy as jnp
from jax import lax
from jax.experimental import pallas as pl
from jax.experimental.pallas import tpu as pltpu
from jax.sharding import PartitionSpec as P

LANES = 128
MIB = 1 << 20
VMEM = pl.BlockSpec(memory_space=pltpu.VMEM)
HBM = pl.BlockSpec(memory_space=pltpu.HBM)


def pack_kernel(slot_hbm, tokens_hbm, ids_hbm, weight_hbm, out_ref, slot_ref, ids_ref, weight_ref, sem):
    rows, width = tokens_hbm.shape
    copies = [
        pltpu.make_async_copy(slot_hbm, slot_ref, sem.at[0]),
        pltpu.make_async_copy(ids_hbm, ids_ref, sem.at[1]),
        pltpu.make_async_copy(weight_hbm, weight_ref, sem.at[2]),
        pltpu.make_async_copy(tokens_hbm, out_ref.at[:, pl.ds(0, width)], sem.at[3]),
    ]
    for copy in copies:
        copy.start()
    for copy in copies:
        copy.wait()
    experts = slot_ref.shape[0]
    extra = out_ref.shape[1] - width
    lane = lax.broadcasted_iota(jnp.int32, (rows, extra), 1)
    ids = ids_ref[...]
    weight = weight_ref[...]
    by_slot = jnp.zeros((rows, extra), jnp.float32)
    slot = jnp.zeros(ids.shape, jnp.int32)
    for e in range(experts):
        slot = jnp.where(ids == e, slot_ref[e], slot)
    for k in range(ids.shape[1]):
        by_slot = by_slot + jnp.where(lane == slot[:, k : k + 1], weight[:, k : k + 1], 0.0)
    high = by_slot.astype(jnp.bfloat16)
    low = by_slot - high.astype(jnp.float32)
    low = pltpu.roll(low, experts, 1)
    columns = jnp.where(lane < experts, high.astype(jnp.float32), low)
    out_ref[:, width:] = columns.astype(jnp.bfloat16)


def join_kernel(*refs):
    row = 0
    for piece in refs[:-1]:
        refs[-1][row : row + piece.shape[0], :] = piece[...]
        row += piece.shape[0]


def join(pieces):
    if len(pieces) == 1:
        return pieces[0]
    rows = sum(piece.shape[0] for piece in pieces)
    width = pieces[0].shape[1]
    return pl.pallas_call(
        join_kernel,
        out_shape=jax.ShapeDtypeStruct((rows, width), jnp.bfloat16),
        in_specs=[VMEM] * len(pieces),
        out_specs=VMEM,
        compiler_params=pltpu.CompilerParams(vmem_limit_bytes=2 * MIB + 8 * rows * width),
        name="join",
    )(*pieces)


def hidden_kernel(units, width, parts, ahead, *refs):
    pieces = refs[:units]
    gate_ref, up_ref, down_ref, hidden_ref, early_ref = refs[units : units + 5]
    x_ref, coef_ref, ring_ref, up_sem, down_sem = refs[units + 5 :]
    slots, _, ff = gate_ref.shape
    experts = coef_ref.shape[2]
    depth = width // parts
    slots_ring = ring_ref.shape[0]
    chunk = early_ref.shape[3]

    def up_copy(step):
        j, p = step // parts, step % parts
        place = lax.rem(step, slots_ring)
        return pltpu.make_async_copy(
            up_ref.at[j, pl.ds(pl.multiple_of(p * depth, depth), depth)], ring_ref.at[place], up_sem.at[place]
        )

    def down_copy(c, j):
        return pltpu.make_async_copy(
            down_ref.at[j, :, pl.ds(c * chunk, chunk)], early_ref.at[c, j], down_sem.at[c, j]
        )

    for step in range(min(slots_ring, slots * parts)):
        up_copy(step).start()
    row = 0
    for piece in pieces:
        count = piece.shape[0]
        x_ref[row : row + count, :] = piece[:, :width]
        coef_ref[0, row : row + count, :] = piece[:, width : width + experts].astype(jnp.float32)
        coef_ref[1, row : row + count, :] = piece[:, width + experts : width + 2 * experts].astype(jnp.float32)
        row += count
    lane = lax.broadcasted_iota(jnp.int32, coef_ref.shape[1:], 1)

    def one(j, carry):
        for c in range(ahead):
            down_copy(c, j).start()
        gate = jnp.dot(x_ref[...], gate_ref[j], preferred_element_type=jnp.float32)
        upper = jnp.zeros(gate.shape, jnp.float32)
        for p in range(parts):
            step = j * parts + p
            up_copy(step).wait()
            upper = upper + jnp.dot(
                x_ref[:, p * depth : (p + 1) * depth],
                ring_ref[lax.rem(step, slots_ring)],
                preferred_element_type=jnp.float32,
            )

            @pl.when(step + slots_ring < slots * parts)
            def _():
                up_copy(step + slots_ring).start()

        own = lane == lax.axis_index("ep") * slots + j
        coef = jnp.sum(jnp.where(own, coef_ref[0] + coef_ref[1], 0.0), axis=1, keepdims=True)
        hidden = gate / (1.0 + jnp.exp(-gate)) * upper * coef
        hidden_ref[:, pl.ds(pl.multiple_of(j * ff, ff), ff)] = hidden.astype(jnp.bfloat16)
        return carry

    lax.fori_loop(0, slots, one, 0)
    for c in range(ahead):
        for j in range(slots):
            down_copy(c, j).wait()


def down_kernel(units, ahead, hidden_ref, early_ref, down_ref, *refs):
    outs = refs[:units]
    late_ref, sem = refs[units:]
    slots, ff, width = down_ref.shape
    chunk = early_ref.shape[3]
    late = late_ref.shape[0]

    def copy(c, j):
        return pltpu.make_async_copy(
            down_ref.at[j, :, pl.ds((ahead + c) * chunk, chunk)], late_ref.at[c, j], sem.at[c, j]
        )

    for c in range(late):
        for j in range(slots):
            copy(c, j).start()
    hidden = hidden_ref[...]
    for c in range(ahead + late):
        if c >= ahead:
            for j in range(slots):
                copy(c - ahead, j).wait()
        block = early_ref[c] if c < ahead else late_ref[c - ahead]
        total = jnp.dot(hidden, block.reshape(slots * ff, chunk), preferred_element_type=jnp.float32)
        total = total.astype(jnp.bfloat16)
        row = 0
        for out in outs:
            count = out.shape[0]
            out[:, c * chunk : (c + 1) * chunk] = total[row : row + count]
            row += count


def add(*terms):
    total = terms[0].astype(jnp.float32)
    for term in terms[1:]:
        total = total + term.astype(jnp.float32)
    return total.astype(jnp.bfloat16)


def in_vmem(value):
    return pltpu.with_memory_space_constraint(value, pltpu.VMEM)


def toward(size, shift):
    return [(i, (i + shift) % size) for i in range(size)]


def body(tokens, expert_ids, combine_weight, slot_of_expert, w_gate, w_up, w_down):
    ep, dp = lax.axis_size("ep"), lax.axis_size("dp")
    core = 2 if dp % 2 == 0 else 1
    chips = dp // core
    rows, width = tokens.shape
    slots, _, ff = w_gate.shape
    experts = slot_of_expert.shape[0]
    extra = -(-2 * experts // LANES) * LANES
    total_rows = rows * ep * dp
    groups = min(ep, 4)

    def step_z(value, shift):
        return lax.ppermute(value, "ep", toward(ep, shift))

    def step_x(value, shift):
        return lax.ppermute(value, "dp", toward(dp, shift * core))

    def step_core(value):
        return lax.ppermute(value, "dp", [(i, i ^ 1) for i in range(dp)])

    packed = pl.pallas_call(
        pack_kernel,
        out_shape=jax.ShapeDtypeStruct((rows, width + extra), jnp.bfloat16),
        in_specs=[HBM] * 4,
        out_specs=VMEM,
        scratch_shapes=[
            pltpu.SMEM(slot_of_expert.shape, jnp.int32),
            pltpu.VMEM(expert_ids.shape, jnp.int32),
            pltpu.VMEM(combine_weight.shape, jnp.float32),
            pltpu.SemaphoreType.DMA((4,)),
        ],
        cost_estimate=pl.CostEstimate(flops=30 * slots * ff * width * 64, bytes_accessed=64 * MIB, transcendentals=0),
        compiler_params=pltpu.CompilerParams(vmem_limit_bytes=2 * MIB),
        name="pack",
    )(*[pltpu.with_memory_space_constraint(value, pltpu.HBM) for value in (slot_of_expert, tokens, expert_ids, combine_weight)])

    along_z = [packed] + [step_z(packed, -s) for s in range(1, ep)]
    per = ep // groups
    along_z = [join(along_z[g * per : (g + 1) * per]) for g in range(groups)]
    along_x = [[step_x(piece, -s) for piece in along_z] for s in range(1, chips)]
    units = [join(along_z)] + [join(pieces) for pieces in along_x]
    if core == 2:
        units += [step_core(unit) for unit in units]
    count = len(units)
    unit_rows = ep * rows

    chunk = next(c for c in (1024, 512, 256, 128, width) if width % c == 0)
    chunks = width // chunk
    ahead = max(1, chunks * 2 // 7)
    parts = 2 if width % 256 == 0 else 1
    ring = min(4, slots * parts)
    gate_in, *held = [in_vmem(value) for value in (w_gate, *units)]
    hidden, early = pl.pallas_call(
        functools.partial(hidden_kernel, count, width, parts, ahead),
        out_shape=(
            pltpu.VMEM((total_rows, slots * ff), jnp.bfloat16),
            pltpu.VMEM((ahead, slots, ff, chunk), jnp.bfloat16),
        ),
        in_specs=[VMEM] * (count + 1) + [HBM, HBM],
        out_specs=(VMEM, VMEM),
        scratch_shapes=[
            pltpu.VMEM((total_rows, width), jnp.bfloat16),
            pltpu.VMEM((2, total_rows, experts), jnp.float32),
            pltpu.VMEM((ring, width // parts, ff), jnp.bfloat16),
            pltpu.SemaphoreType.DMA((ring,)),
            pltpu.SemaphoreType.DMA((ahead, slots)),
        ],
        cost_estimate=pl.CostEstimate(
            flops=4 * total_rows * slots * ff * width,
            bytes_accessed=6 * slots * ff * width,
            transcendentals=total_rows * slots * ff,
        ),
        compiler_params=pltpu.CompilerParams(vmem_limit_bytes=21 * MIB),
        name="hidden",
    )(*held, gate_in, w_up, w_down)

    outs = pl.pallas_call(
        functools.partial(down_kernel, count, ahead),
        out_shape=[jax.ShapeDtypeStruct((unit_rows, width), jnp.bfloat16)] * count,
        in_specs=[VMEM, VMEM, HBM],
        out_specs=[VMEM] * count,
        scratch_shapes=[
            pltpu.VMEM((chunks - ahead, slots, ff, chunk), jnp.bfloat16),
            pltpu.SemaphoreType.DMA((chunks - ahead, slots)),
        ],
        cost_estimate=pl.CostEstimate(
            flops=2 * total_rows * slots * ff * width, bytes_accessed=2 * slots * ff * width, transcendentals=0
        ),
        compiler_params=pltpu.CompilerParams(vmem_limit_bytes=40 * MIB),
        name="down",
    )(hidden, early, w_down)

    terms = [[value] for value in outs[:chips]]
    if core == 2:
        for s in list(range(1, chips)) + [0]:
            terms[s].append(step_core(outs[chips + s]))
    near = terms[0] + [step_x(add(*terms[s]), s) for s in range(1, chips)]
    pieces = [add(*[term[s * rows : (s + 1) * rows] for term in near]) for s in range(ep)]
    return add(pieces[0], *[step_z(pieces[s], s) for s in range(1, ep)])


def solution(mesh):
    in_specs = (
        P(("grp", "ep", "dp"), None),
        P(("grp", "ep", "dp"), None),
        P(("grp", "ep", "dp"), None),
        P(),
        P("ep", None, "dp"),
        P("ep", None, "dp"),
        P("ep", "dp", None),
    )
    out_specs = P(("grp", "ep", "dp"), None)
    return jax.shard_map(body, mesh=mesh, in_specs=in_specs, out_specs=out_specs, check_vma=False)
```

```python
import functools

import jax
import jax.numpy as jnp
from jax import lax
from jax.experimental import pallas as pl
from jax.experimental.pallas import tpu as pltpu
from jax.sharding import PartitionSpec as P

LANES = 128
MIB = 1 << 20
RING = 2
BLOCKS = 4
LIMIT = 30
VMEM = pl.BlockSpec(memory_space=pltpu.VMEM)
HBM = pl.BlockSpec(memory_space=pltpu.HBM)


def pack_kernel(slot_hbm, tokens_hbm, ids_hbm, weight_hbm, out_ref, slot_ref, ids_ref, weight_ref, sem):
    rows, width = tokens_hbm.shape
    copies = [
        pltpu.make_async_copy(slot_hbm, slot_ref, sem.at[0]),
        pltpu.make_async_copy(ids_hbm, ids_ref, sem.at[1]),
        pltpu.make_async_copy(weight_hbm, weight_ref, sem.at[2]),
        pltpu.make_async_copy(tokens_hbm, out_ref.at[:, pl.ds(0, width)], sem.at[3]),
    ]
    for copy in copies:
        copy.start()
    for copy in copies:
        copy.wait()
    experts = slot_ref.shape[0]
    extra = out_ref.shape[1] - width
    lane = lax.broadcasted_iota(jnp.int32, (rows, extra), 1)
    ids = ids_ref[...]
    weight = weight_ref[...]
    by_slot = jnp.zeros((rows, extra), jnp.float32)
    slot = jnp.zeros(ids.shape, jnp.int32)
    for e in range(experts):
        slot = jnp.where(ids == e, slot_ref[e], slot)
    for k in range(ids.shape[1]):
        by_slot = by_slot + jnp.where(lane == slot[:, k : k + 1], weight[:, k : k + 1], 0.0)
    high = by_slot.astype(jnp.bfloat16)
    low = by_slot - high.astype(jnp.float32)
    low = pltpu.roll(low, experts, 1)
    columns = jnp.where(lane < experts, high.astype(jnp.float32), low)
    out_ref[:, width:] = columns.astype(jnp.bfloat16)


def join_kernel(*refs):
    row = 0
    for piece in refs[:-1]:
        refs[-1][row : row + piece.shape[0], :] = piece[...]
        row += piece.shape[0]


def join(pieces):
    if len(pieces) == 1:
        return pieces[0]
    rows = sum(piece.shape[0] for piece in pieces)
    width = pieces[0].shape[1]
    return pl.pallas_call(
        join_kernel,
        out_shape=jax.ShapeDtypeStruct((rows, width), jnp.bfloat16),
        in_specs=[VMEM] * len(pieces),
        out_specs=VMEM,
        compiler_params=pltpu.CompilerParams(vmem_limit_bytes=2 * MIB + 8 * rows * width),
        name="join",
    )(*pieces)


def expert_kernel(units, parts, chunk, *refs):
    pieces = refs[:units]
    gate_ref, up_ref, down_ref = refs[units : units + 3]
    outs = refs[units + 3 : 2 * units + 3]
    x_ref, coef_ref, hidden_ref, ring_ref, block_ref, up_sem, down_sem = refs[2 * units + 3 :]
    slots, width, ff = gate_ref.shape
    experts = coef_ref.shape[2]
    depth = width // parts
    steps = slots * parts
    ring = ring_ref.shape[0]
    chunks = width // chunk
    blocks = block_ref.shape[0]

    def up_copy(step):
        j, p = step // parts, step % parts
        place = lax.rem(step, ring)
        return pltpu.make_async_copy(
            up_ref.at[j, pl.ds(pl.multiple_of(p * depth, depth), depth)], ring_ref.at[place], up_sem.at[place]
        )

    def down_copy(c, j):
        return pltpu.make_async_copy(
            down_ref.at[j, :, pl.ds(c * chunk, chunk)], block_ref.at[c % blocks, j], down_sem.at[c % blocks, j]
        )

    for step in range(ring):
        up_copy(step).start()
    row = 0
    for piece in pieces:
        count = piece.shape[0]
        x_ref[row : row + count, :] = piece[:, :width]
        coef_ref[0, row : row + count, :] = piece[:, width : width + experts].astype(jnp.float32)
        coef_ref[1, row : row + count, :] = piece[:, width + experts : width + 2 * experts].astype(jnp.float32)
        row += count
    lane = lax.broadcasted_iota(jnp.int32, coef_ref.shape[1:], 1)

    def one(j, carry):
        for c in range(blocks):
            down_copy(c, j).start()
        gate = jnp.dot(x_ref[...], gate_ref[j], preferred_element_type=jnp.float32)
        upper = jnp.zeros(gate.shape, jnp.float32)
        for p in range(parts):
            step = j * parts + p
            up_copy(step).wait()
            upper = upper + jnp.dot(
                x_ref[:, p * depth : (p + 1) * depth],
                ring_ref[lax.rem(step, ring)],
                preferred_element_type=jnp.float32,
            )

            @pl.when(step + ring < steps)
            def _():
                up_copy(step + ring).start()

        own = lane == lax.axis_index("ep") * slots + j
        coef = jnp.sum(jnp.where(own, coef_ref[0] + coef_ref[1], 0.0), axis=1, keepdims=True)
        hidden = gate / (1.0 + jnp.exp(-gate)) * upper * coef
        hidden_ref[:, pl.ds(pl.multiple_of(j * ff, ff), ff)] = hidden.astype(jnp.bfloat16)
        return carry

    lax.fori_loop(0, slots, one, 0)
    for c in range(chunks):
        for j in range(slots):
            down_copy(c, j).wait()
        block = block_ref[c % blocks].reshape(slots * ff, chunk)
        total = jnp.dot(hidden_ref[...], block, preferred_element_type=jnp.float32).astype(jnp.bfloat16)
        if c + blocks < chunks:
            for j in range(slots):
                down_copy(c + blocks, j).start()
        row = 0
        for out in outs:
            count = out.shape[0]
            out[:, c * chunk : (c + 1) * chunk] = total[row : row + count]
            row += count


def add(*terms):
    total = terms[0].astype(jnp.float32)
    for term in terms[1:]:
        total = total + term.astype(jnp.float32)
    return total.astype(jnp.bfloat16)


def in_vmem(value):
    return pltpu.with_memory_space_constraint(value, pltpu.VMEM)


def toward(size, shift):
    return [(i, (i + shift) % size) for i in range(size)]


def body(tokens, expert_ids, combine_weight, slot_of_expert, w_gate, w_up, w_down):
    ep, dp = lax.axis_size("ep"), lax.axis_size("dp")
    core = 2 if dp % 2 == 0 else 1
    chips = dp // core
    rows, width = tokens.shape
    slots, _, ff = w_gate.shape
    experts = slot_of_expert.shape[0]
    extra = -(-2 * experts // LANES) * LANES
    total_rows = rows * ep * dp
    groups = min(ep, 4)

    def step_z(value, shift):
        return lax.ppermute(value, "ep", toward(ep, shift))

    def step_x(value, shift):
        return lax.ppermute(value, "dp", toward(dp, shift * core))

    def step_core(value):
        return lax.ppermute(value, "dp", [(i, i ^ 1) for i in range(dp)])

    packed = pl.pallas_call(
        pack_kernel,
        out_shape=jax.ShapeDtypeStruct((rows, width + extra), jnp.bfloat16),
        in_specs=[HBM] * 4,
        out_specs=VMEM,
        scratch_shapes=[
            pltpu.SMEM(slot_of_expert.shape, jnp.int32),
            pltpu.VMEM(expert_ids.shape, jnp.int32),
            pltpu.VMEM(combine_weight.shape, jnp.float32),
            pltpu.SemaphoreType.DMA((4,)),
        ],
        cost_estimate=pl.CostEstimate(flops=30 * slots * ff * width * 64, bytes_accessed=64 * MIB, transcendentals=0),
        compiler_params=pltpu.CompilerParams(vmem_limit_bytes=2 * MIB),
        name="pack",
    )(*[pltpu.with_memory_space_constraint(value, pltpu.HBM) for value in (slot_of_expert, tokens, expert_ids, combine_weight)])

    along_z = [packed] + [step_z(packed, -s) for s in range(1, ep)]
    per = ep // groups
    along_z = [join(along_z[g * per : (g + 1) * per]) for g in range(groups)]
    along_x = [[step_x(piece, -s) for piece in along_z] for s in range(1, chips)]
    units = [join(along_z)] + [join(pieces) for pieces in along_x]
    if core == 2:
        units += [step_core(unit) for unit in units]
    count = len(units)
    unit_rows = ep * rows

    chunk = next(c for c in (1024, 512, 256, 128, width) if width % c == 0)
    blocks = min(BLOCKS, width // chunk)
    parts = 2 if width % 256 == 0 else 1
    ring = min(RING, slots * parts)
    outs = pl.pallas_call(
        functools.partial(expert_kernel, count, parts, chunk),
        out_shape=[pltpu.VMEM((unit_rows, width), jnp.bfloat16)] * count,
        in_specs=[VMEM] * (count + 1) + [HBM, HBM],
        out_specs=[VMEM] * count,
        scratch_shapes=[
            pltpu.VMEM((total_rows, width), jnp.bfloat16),
            pltpu.VMEM((2, total_rows, experts), jnp.float32),
            pltpu.VMEM((total_rows, slots * ff), jnp.bfloat16),
            pltpu.VMEM((ring, width // parts, ff), jnp.bfloat16),
            pltpu.VMEM((blocks, slots, ff, chunk), jnp.bfloat16),
            pltpu.SemaphoreType.DMA((ring,)),
            pltpu.SemaphoreType.DMA((blocks, slots)),
        ],
        cost_estimate=pl.CostEstimate(
            flops=6 * total_rows * slots * ff * width,
            bytes_accessed=6 * slots * ff * width,
            transcendentals=total_rows * slots * ff,
        ),
        compiler_params=pltpu.CompilerParams(vmem_limit_bytes=LIMIT * MIB),
        name="expert",
    )(*[in_vmem(value) for value in (*units, w_gate)], w_up, w_down)

    terms = [[value] for value in outs[:chips]]
    if core == 2:
        for s in list(range(1, chips)) + [0]:
            terms[s].append(step_core(outs[chips + s]))
    near = terms[0] + [step_x(add(*terms[s]), s) for s in range(1, chips)]
    pieces = [add(*[term[s * rows : (s + 1) * rows] for term in near]) for s in range(ep)]
    return add(pieces[0], *[step_z(pieces[s], s) for s in range(1, ep)])


def solution(mesh):
    in_specs = (
        P(("grp", "ep", "dp"), None),
        P(("grp", "ep", "dp"), None),
        P(("grp", "ep", "dp"), None),
        P(),
        P("ep", None, "dp"),
        P("ep", None, "dp"),
        P("ep", "dp", None),
    )
    out_specs = P(("grp", "ep", "dp"), None)
    return jax.shard_map(body, mesh=mesh, in_specs=in_specs, out_specs=out_specs, check_vma=False)
```

```python
import functools

import jax
import jax.numpy as jnp
from jax import lax
from jax.experimental import pallas as pl
from jax.experimental.pallas import tpu as pltpu
from jax.sharding import PartitionSpec as P

LANES = 128
MIB = 1 << 20
RING = 2
BLOCKS = 4
LIMIT = 30
VMEM = pl.BlockSpec(memory_space=pltpu.VMEM)
HBM = pl.BlockSpec(memory_space=pltpu.HBM)


def pack_kernel(slot_hbm, tokens_hbm, ids_hbm, weight_hbm, out_ref, slot_ref, ids_ref, weight_ref, sem):
    rows, width = tokens_hbm.shape
    copies = [
        pltpu.make_async_copy(slot_hbm, slot_ref, sem.at[0]),
        pltpu.make_async_copy(ids_hbm, ids_ref, sem.at[1]),
        pltpu.make_async_copy(weight_hbm, weight_ref, sem.at[2]),
        pltpu.make_async_copy(tokens_hbm, out_ref.at[:, pl.ds(0, width)], sem.at[3]),
    ]
    for copy in copies:
        copy.start()
    for copy in copies:
        copy.wait()
    experts = slot_ref.shape[0]
    extra = out_ref.shape[1] - width
    lane = lax.broadcasted_iota(jnp.int32, (rows, extra), 1)
    ids = ids_ref[...]
    weight = weight_ref[...]
    by_slot = jnp.zeros((rows, extra), jnp.float32)
    slot = jnp.zeros(ids.shape, jnp.int32)
    for e in range(experts):
        slot = jnp.where(ids == e, slot_ref[e], slot)
    for k in range(ids.shape[1]):
        by_slot = by_slot + jnp.where(lane == slot[:, k : k + 1], weight[:, k : k + 1], 0.0)
    high = by_slot.astype(jnp.bfloat16)
    low = by_slot - high.astype(jnp.float32)
    low = pltpu.roll(low, experts, 1)
    columns = jnp.where(lane < experts, high.astype(jnp.float32), low)
    out_ref[:, width:] = columns.astype(jnp.bfloat16)


def join_kernel(*refs):
    row = 0
    for piece in refs[:-1]:
        refs[-1][row : row + piece.shape[0], :] = piece[...]
        row += piece.shape[0]


def join(pieces):
    if len(pieces) == 1:
        return pieces[0]
    rows = sum(piece.shape[0] for piece in pieces)
    width = pieces[0].shape[1]
    return pl.pallas_call(
        join_kernel,
        out_shape=jax.ShapeDtypeStruct((rows, width), jnp.bfloat16),
        in_specs=[VMEM] * len(pieces),
        out_specs=VMEM,
        compiler_params=pltpu.CompilerParams(vmem_limit_bytes=2 * MIB + 8 * rows * width),
        name="join",
    )(*pieces)


def expert_kernel(units, parts, chunk, *refs):
    pieces = refs[:units]
    gate_ref, up_ref, down_ref = refs[units : units + 3]
    outs = refs[units + 3 : 2 * units + 3]
    x_ref, coef_ref, hidden_ref, ring_ref, block_ref, up_sem, down_sem = refs[2 * units + 3 :]
    slots, width, ff = gate_ref.shape
    experts = coef_ref.shape[2]
    depth = width // parts
    steps = slots * parts
    ring = ring_ref.shape[0]
    chunks = width // chunk
    blocks = block_ref.shape[0]

    def up_copy(step):
        j, p = step // parts, step % parts
        place = lax.rem(step, ring)
        return pltpu.make_async_copy(
            up_ref.at[j, pl.ds(pl.multiple_of(p * depth, depth), depth)], ring_ref.at[place], up_sem.at[place]
        )

    def down_copy(c, j):
        return pltpu.make_async_copy(
            down_ref.at[j, :, pl.ds(c * chunk, chunk)], block_ref.at[c % blocks, j], down_sem.at[c % blocks, j]
        )

    for step in range(ring):
        up_copy(step).start()
    row = 0
    for piece in pieces:
        count = piece.shape[0]
        x_ref[row : row + count, :] = piece[:, :width]
        coef_ref[0, row : row + count, :] = piece[:, width : width + experts].astype(jnp.float32)
        coef_ref[1, row : row + count, :] = piece[:, width + experts : width + 2 * experts].astype(jnp.float32)
        row += count
    lane = lax.broadcasted_iota(jnp.int32, coef_ref.shape[1:], 1)

    def one(j, carry):
        for c in range(blocks):
            down_copy(c, j).start()
        gate = jnp.dot(x_ref[...], gate_ref[j], preferred_element_type=jnp.float32)
        upper = jnp.zeros(gate.shape, jnp.float32)
        for p in range(parts):
            step = j * parts + p
            up_copy(step).wait()
            upper = upper + jnp.dot(
                x_ref[:, p * depth : (p + 1) * depth],
                ring_ref[lax.rem(step, ring)],
                preferred_element_type=jnp.float32,
            )

            @pl.when(step + ring < steps)
            def _():
                up_copy(step + ring).start()

        own = lane == lax.axis_index("ep") * slots + j
        coef = jnp.sum(jnp.where(own, coef_ref[0] + coef_ref[1], 0.0), axis=1, keepdims=True)
        hidden = gate / (1.0 + jnp.exp(-gate)) * upper * coef
        hidden_ref[:, pl.ds(pl.multiple_of(j * ff, ff), ff)] = hidden.astype(jnp.bfloat16)
        return carry

    lax.fori_loop(0, slots, one, 0)
    for c in range(chunks):
        for j in range(slots):
            down_copy(c, j).wait()
        block = block_ref[c % blocks].reshape(slots * ff, chunk)
        total = jnp.dot(hidden_ref[...], block, preferred_element_type=jnp.float32).astype(jnp.bfloat16)
        if c + blocks < chunks:
            for j in range(slots):
                down_copy(c + blocks, j).start()
        row = 0
        for out in outs:
            count = out.shape[0]
            out[:, c * chunk : (c + 1) * chunk] = total[row : row + count]
            row += count


def add_kernel(starts, *refs):
    count = refs[-1].shape[0]
    total = None
    for start, ref in zip(starts, refs[:-1]):
        term = ref[start : start + count, :].astype(jnp.float32)
        total = term if total is None else total + term
    refs[-1][...] = total.astype(jnp.bfloat16)


def add(terms, count):
    width = terms[0][0].shape[1]
    return pl.pallas_call(
        functools.partial(add_kernel, [start for _, start in terms]),
        out_shape=jax.ShapeDtypeStruct((count, width), jnp.bfloat16),
        in_specs=[VMEM] * len(terms),
        out_specs=VMEM,
        compiler_params=pltpu.CompilerParams(vmem_limit_bytes=2 * MIB + 32 * count * width),
        name="add",
    )(*[value for value, _ in terms])


def in_vmem(value):
    return pltpu.with_memory_space_constraint(value, pltpu.VMEM)


def toward(size, shift):
    return [(i, (i + shift) % size) for i in range(size)]


def body(tokens, expert_ids, combine_weight, slot_of_expert, w_gate, w_up, w_down):
    ep, dp = lax.axis_size("ep"), lax.axis_size("dp")
    core = 2 if dp % 2 == 0 else 1
    chips = dp // core
    rows, width = tokens.shape
    slots, _, ff = w_gate.shape
    experts = slot_of_expert.shape[0]
    extra = -(-2 * experts // LANES) * LANES
    total_rows = rows * ep * dp
    groups = min(ep, 4)

    def step_z(value, shift):
        return lax.ppermute(value, "ep", toward(ep, shift))

    def step_x(value, shift):
        return lax.ppermute(value, "dp", toward(dp, shift * core))

    def step_core(value):
        return lax.ppermute(value, "dp", [(i, i ^ 1) for i in range(dp)])

    packed = pl.pallas_call(
        pack_kernel,
        out_shape=jax.ShapeDtypeStruct((rows, width + extra), jnp.bfloat16),
        in_specs=[HBM] * 4,
        out_specs=VMEM,
        scratch_shapes=[
            pltpu.SMEM(slot_of_expert.shape, jnp.int32),
            pltpu.VMEM(expert_ids.shape, jnp.int32),
            pltpu.VMEM(combine_weight.shape, jnp.float32),
            pltpu.SemaphoreType.DMA((4,)),
        ],
        cost_estimate=pl.CostEstimate(flops=30 * slots * ff * width * 64, bytes_accessed=64 * MIB, transcendentals=0),
        compiler_params=pltpu.CompilerParams(vmem_limit_bytes=2 * MIB),
        name="pack",
    )(*[pltpu.with_memory_space_constraint(value, pltpu.HBM) for value in (slot_of_expert, tokens, expert_ids, combine_weight)])

    along_z = [packed] + [step_z(packed, -s) for s in range(1, ep)]
    per = ep // groups
    along_z = [join(along_z[g * per : (g + 1) * per]) for g in range(groups)]
    along_x = [[step_x(piece, -s) for piece in along_z] for s in range(1, chips)]
    units = [join(along_z)] + [join(pieces) for pieces in along_x]
    if core == 2:
        units += [step_core(unit) for unit in units]
    count = len(units)
    unit_rows = ep * rows

    chunk = next(c for c in (1024, 512, 256, 128, width) if width % c == 0)
    blocks = min(BLOCKS, width // chunk)
    parts = 2 if width % 256 == 0 else 1
    ring = min(RING, slots * parts)
    outs = pl.pallas_call(
        functools.partial(expert_kernel, count, parts, chunk),
        out_shape=[pltpu.VMEM((unit_rows, width), jnp.bfloat16)] * count,
        in_specs=[VMEM] * (count + 1) + [HBM, HBM],
        out_specs=[VMEM] * count,
        scratch_shapes=[
            pltpu.VMEM((total_rows, width), jnp.bfloat16),
            pltpu.VMEM((2, total_rows, experts), jnp.float32),
            pltpu.VMEM((total_rows, slots * ff), jnp.bfloat16),
            pltpu.VMEM((ring, width // parts, ff), jnp.bfloat16),
            pltpu.VMEM((blocks, slots, ff, chunk), jnp.bfloat16),
            pltpu.SemaphoreType.DMA((ring,)),
            pltpu.SemaphoreType.DMA((blocks, slots)),
        ],
        cost_estimate=pl.CostEstimate(
            flops=6 * total_rows * slots * ff * width,
            bytes_accessed=6 * slots * ff * width,
            transcendentals=total_rows * slots * ff,
        ),
        compiler_params=pltpu.CompilerParams(vmem_limit_bytes=LIMIT * MIB),
        name="expert",
    )(*[in_vmem(value) for value in (*units, w_gate)], w_up, w_down)

    near, far = outs[:chips], outs[chips:]
    moved = [None] * chips
    if core == 2:
        for s in list(range(1, chips)) + [0]:
            moved[s] = step_core(far[s])

    def here(s, row):
        return [(value[s], row) for value in (near, moved) if value[s] is not None]

    size = per * rows
    order = list(range(1, groups)) + [0]
    arrived = {g: [step_x(add(here(s, g * size), size), s) for s in range(1, chips)] for g in order}

    def piece(s):
        g, row = s // per, s % per * rows
        return here(0, s * rows) + [(value, row) for value in arrived[g]]

    returned = [(step_z(add(piece(s), rows), s), 0) for s in range(1, ep)]
    return add(piece(0) + returned, rows)


def solution(mesh):
    in_specs = (
        P(("grp", "ep", "dp"), None),
        P(("grp", "ep", "dp"), None),
        P(("grp", "ep", "dp"), None),
        P(),
        P("ep", None, "dp"),
        P("ep", None, "dp"),
        P("ep", "dp", None),
    )
    out_specs = P(("grp", "ep", "dp"), None)
    return jax.shard_map(body, mesh=mesh, in_specs=in_specs, out_specs=out_specs, check_vma=False)
```

```python
import functools

import jax
import jax.numpy as jnp
from jax import lax
from jax.experimental import pallas as pl
from jax.experimental.pallas import tpu as pltpu
from jax.sharding import PartitionSpec as P

LANES = 128
MIB = 1 << 20
RING = 2
BLOCKS = 4
LIMIT = 26
VMEM = pl.BlockSpec(memory_space=pltpu.VMEM)
HBM = pl.BlockSpec(memory_space=pltpu.HBM)
ANY = pl.BlockSpec(memory_space=pl.ANY)


def pack_kernel(slot_hbm, tokens_hbm, ids_hbm, weight_hbm, out_ref, slot_ref, ids_ref, weight_ref, sem):
    rows, width = tokens_hbm.shape
    copies = [
        pltpu.make_async_copy(slot_hbm, slot_ref, sem.at[0]),
        pltpu.make_async_copy(ids_hbm, ids_ref, sem.at[1]),
        pltpu.make_async_copy(weight_hbm, weight_ref, sem.at[2]),
        pltpu.make_async_copy(tokens_hbm, out_ref.at[:, pl.ds(0, width)], sem.at[3]),
    ]
    for copy in copies:
        copy.start()
    for copy in copies:
        copy.wait()
    experts = slot_ref.shape[0]
    extra = out_ref.shape[1] - width
    lane = lax.broadcasted_iota(jnp.int32, (rows, extra), 1)
    ids = ids_ref[...]
    weight = weight_ref[...]
    by_slot = jnp.zeros((rows, extra), jnp.float32)
    slot = jnp.zeros(ids.shape, jnp.int32)
    for e in range(experts):
        slot = jnp.where(ids == e, slot_ref[e], slot)
    for k in range(ids.shape[1]):
        by_slot = by_slot + jnp.where(lane == slot[:, k : k + 1], weight[:, k : k + 1], 0.0)
    high = by_slot.astype(jnp.bfloat16)
    low = by_slot - high.astype(jnp.float32)
    low = pltpu.roll(low, experts, 1)
    columns = jnp.where(lane < experts, high.astype(jnp.float32), low)
    out_ref[:, width:] = columns.astype(jnp.bfloat16)


def join_kernel(*refs):
    row = 0
    for piece in refs[:-1]:
        refs[-1][row : row + piece.shape[0], :] = piece[...]
        row += piece.shape[0]


def join_fetch_kernel(parts, units, *refs):
    pieces = refs[:units]
    up_ref, _, out_ref, ring_ref, held_ref, piece_sem, sem = refs[units:]
    ring, depth, _ = ring_ref.shape
    moves = [
        pltpu.make_async_copy(piece, held_ref.at[u], piece_sem.at[u]) for u, piece in enumerate(pieces)
    ]
    copies = [
        pltpu.make_async_copy(
            up_ref.at[step // parts, pl.ds(step % parts * depth, depth)], ring_ref.at[step], sem.at[step]
        )
        for step in range(ring)
    ]
    for copy in moves + copies:
        copy.start()
    rows = held_ref.shape[1]
    for u, move in enumerate(moves):
        move.wait()
        out_ref[u * rows : (u + 1) * rows, :] = held_ref[u]
    for copy in copies:
        copy.wait()


def join(pieces):
    if len(pieces) == 1:
        return pieces[0]
    rows = sum(piece.shape[0] for piece in pieces)
    width = pieces[0].shape[1]
    return pl.pallas_call(
        join_kernel,
        out_shape=jax.ShapeDtypeStruct((rows, width), jnp.bfloat16),
        in_specs=[VMEM] * len(pieces),
        out_specs=VMEM,
        compiler_params=pltpu.CompilerParams(vmem_limit_bytes=2 * MIB + 8 * rows * width),
        name="join",
    )(*pieces)


def join_fetch(pieces, w_up, held, parts, ring):
    rows = sum(piece.shape[0] for piece in pieces)
    width = pieces[0].shape[1]
    _, depth, ff = w_up.shape
    return pl.pallas_call(
        functools.partial(join_fetch_kernel, parts, len(pieces)),
        out_shape=(
            pltpu.VMEM((rows, width), jnp.bfloat16),
            pltpu.VMEM((ring, depth // parts, ff), jnp.bfloat16),
        ),
        in_specs=[ANY] * len(pieces) + [HBM, VMEM],
        out_specs=(VMEM, VMEM),
        scratch_shapes=[
            pltpu.VMEM((len(pieces), *pieces[0].shape), jnp.bfloat16),
            pltpu.SemaphoreType.DMA((len(pieces),)),
            pltpu.SemaphoreType.DMA((ring,)),
        ],
        compiler_params=pltpu.CompilerParams(vmem_limit_bytes=LIMIT * MIB),
        name="fetch",
    )(*pieces, w_up, held)


def expert_kernel(units, parts, chunk, *refs):
    pieces = refs[:units]
    gate_ref, _, up_ref, down_ref = refs[units : units + 4]
    outs = refs[units + 4 : 2 * units + 4]
    ring_ref, x_ref, coef_ref, hidden_ref, block_ref, up_sem, down_sem = refs[2 * units + 4 :]
    slots, width, ff = gate_ref.shape
    experts = coef_ref.shape[2]
    depth = width // parts
    steps = slots * parts
    ring = ring_ref.shape[0]
    chunks = width // chunk
    blocks = block_ref.shape[0]

    def up_copy(step):
        j, p = step // parts, step % parts
        place = lax.rem(step, ring)
        return pltpu.make_async_copy(
            up_ref.at[j, pl.ds(pl.multiple_of(p * depth, depth), depth)], ring_ref.at[place], up_sem.at[place]
        )

    def down_copy(c, j):
        return pltpu.make_async_copy(
            down_ref.at[j, :, pl.ds(c * chunk, chunk)], block_ref.at[c % blocks, j], down_sem.at[c % blocks, j]
        )

    row = 0
    for piece in pieces:
        count = piece.shape[0]
        x_ref[row : row + count, :] = piece[:, :width]
        coef_ref[0, row : row + count, :] = piece[:, width : width + experts].astype(jnp.float32)
        coef_ref[1, row : row + count, :] = piece[:, width + experts : width + 2 * experts].astype(jnp.float32)
        row += count
    lane = lax.broadcasted_iota(jnp.int32, coef_ref.shape[1:], 1)

    def one(j, carry):
        for c in range(blocks):
            down_copy(c, j).start()
        gate = jnp.dot(x_ref[...], gate_ref[j], preferred_element_type=jnp.float32)
        upper = jnp.zeros(gate.shape, jnp.float32)
        for p in range(parts):
            step = j * parts + p

            @pl.when(step >= ring)
            def _():
                up_copy(step).wait()

            upper = upper + jnp.dot(
                x_ref[:, p * depth : (p + 1) * depth],
                ring_ref[lax.rem(step, ring)],
                preferred_element_type=jnp.float32,
            )

            @pl.when(step + ring < steps)
            def _():
                up_copy(step + ring).start()

        own = lane == lax.axis_index("ep") * slots + j
        coef = jnp.sum(jnp.where(own, coef_ref[0] + coef_ref[1], 0.0), axis=1, keepdims=True)
        hidden = gate / (1.0 + jnp.exp(-gate)) * upper * coef
        hidden_ref[:, pl.ds(pl.multiple_of(j * ff, ff), ff)] = hidden.astype(jnp.bfloat16)
        return carry

    lax.fori_loop(0, slots, one, 0)
    for c in range(chunks):
        for j in range(slots):
            down_copy(c, j).wait()
        block = block_ref[c % blocks].reshape(slots * ff, chunk)
        total = jnp.dot(hidden_ref[...], block, preferred_element_type=jnp.float32).astype(jnp.bfloat16)
        if c + blocks < chunks:
            for j in range(slots):
                down_copy(c + blocks, j).start()
        row = 0
        for out in outs:
            count = out.shape[0]
            out[:, c * chunk : (c + 1) * chunk] = total[row : row + count]
            row += count


def add_kernel(starts, *refs):
    count = refs[-1].shape[0]
    total = None
    for start, ref in zip(starts, refs[:-1]):
        term = ref[start : start + count, :].astype(jnp.float32)
        total = term if total is None else total + term
    refs[-1][...] = total.astype(jnp.bfloat16)


def add(terms, count):
    width = terms[0][0].shape[1]
    return pl.pallas_call(
        functools.partial(add_kernel, [start for _, start in terms]),
        out_shape=jax.ShapeDtypeStruct((count, width), jnp.bfloat16),
        in_specs=[VMEM] * len(terms),
        out_specs=VMEM,
        compiler_params=pltpu.CompilerParams(vmem_limit_bytes=2 * MIB + 32 * count * width),
        name="add",
    )(*[value for value, _ in terms])


def in_vmem(value):
    return pltpu.with_memory_space_constraint(value, pltpu.VMEM)


def toward(size, shift):
    return [(i, (i + shift) % size) for i in range(size)]


def body(tokens, expert_ids, combine_weight, slot_of_expert, w_gate, w_up, w_down):
    ep, dp = lax.axis_size("ep"), lax.axis_size("dp")
    core = 2 if dp % 2 == 0 else 1
    chips = dp // core
    rows, width = tokens.shape
    slots, _, ff = w_gate.shape
    experts = slot_of_expert.shape[0]
    extra = -(-2 * experts // LANES) * LANES
    total_rows = rows * ep * dp
    groups = min(ep, 4)

    def step_z(value, shift):
        return lax.ppermute(value, "ep", toward(ep, shift))

    def step_x(value, shift):
        return lax.ppermute(value, "dp", toward(dp, shift * core))

    def step_core(value):
        return lax.ppermute(value, "dp", [(i, i ^ 1) for i in range(dp)])

    packed = pl.pallas_call(
        pack_kernel,
        out_shape=jax.ShapeDtypeStruct((rows, width + extra), jnp.bfloat16),
        in_specs=[HBM] * 4,
        out_specs=VMEM,
        scratch_shapes=[
            pltpu.SMEM(slot_of_expert.shape, jnp.int32),
            pltpu.VMEM(expert_ids.shape, jnp.int32),
            pltpu.VMEM(combine_weight.shape, jnp.float32),
            pltpu.SemaphoreType.DMA((4,)),
        ],
        cost_estimate=pl.CostEstimate(flops=30 * slots * ff * width * 64, bytes_accessed=64 * MIB, transcendentals=0),
        compiler_params=pltpu.CompilerParams(vmem_limit_bytes=2 * MIB),
        name="pack",
    )(*[pltpu.with_memory_space_constraint(value, pltpu.HBM) for value in (slot_of_expert, tokens, expert_ids, combine_weight)])

    along_z = [packed] + [step_z(packed, -s) for s in range(1, ep)]
    per = ep // groups
    along_z = [join(along_z[g * per : (g + 1) * per]) for g in range(groups)]
    along_x = [[step_x(piece, -s) for piece in along_z] for s in range(1, chips)]
    parts = 2 if width % 256 == 0 else 1
    ring = min(RING, slots * parts)
    gate_in = in_vmem(w_gate)
    joined, fetched = join_fetch(along_z, w_up, gate_in, parts, ring)
    units = [joined] + [join(pieces) for pieces in along_x]
    if core == 2:
        units += [step_core(unit) for unit in units]
    count = len(units)
    unit_rows = ep * rows

    chunk = next(c for c in (1024, 512, 256, 128, width) if width % c == 0)
    blocks = min(BLOCKS, width // chunk)
    *outs, _ = pl.pallas_call(
        functools.partial(expert_kernel, count, parts, chunk),
        out_shape=[pltpu.VMEM((unit_rows, width), jnp.bfloat16)] * count
        + [pltpu.VMEM((ring, width // parts, ff), jnp.bfloat16)],
        in_specs=[VMEM] * (count + 2) + [HBM, HBM],
        out_specs=[VMEM] * (count + 1),
        input_output_aliases={count + 1: count},
        scratch_shapes=[
            pltpu.VMEM((total_rows, width), jnp.bfloat16),
            pltpu.VMEM((2, total_rows, experts), jnp.float32),
            pltpu.VMEM((total_rows, slots * ff), jnp.bfloat16),
            pltpu.VMEM((blocks, slots, ff, chunk), jnp.bfloat16),
            pltpu.SemaphoreType.DMA((ring,)),
            pltpu.SemaphoreType.DMA((blocks, slots)),
        ],
        cost_estimate=pl.CostEstimate(
            flops=6 * total_rows * slots * ff * width,
            bytes_accessed=6 * slots * ff * width,
            transcendentals=total_rows * slots * ff,
        ),
        compiler_params=pltpu.CompilerParams(vmem_limit_bytes=LIMIT * MIB),
        name="expert",
    )(*[in_vmem(value) for value in units], gate_in, in_vmem(fetched), w_up, w_down)

    near, far = outs[:chips], outs[chips:]
    moved = [None] * chips
    if core == 2:
        for s in list(range(1, chips)) + [0]:
            moved[s] = step_core(far[s])

    def here(s, row):
        return [(value[s], row) for value in (near, moved) if value[s] is not None]

    size = per * rows
    order = list(range(1, groups)) + [0]
    arrived = {g: [step_x(add(here(s, g * size), size), s) for s in range(1, chips)] for g in order}

    def piece(s):
        g, row = s // per, s % per * rows
        return here(0, s * rows) + [(value, row) for value in arrived[g]]

    returned = [(step_z(add(piece(s), rows), s), 0) for s in range(1, ep)]
    return add(piece(0) + returned, rows)


def solution(mesh):
    in_specs = (
        P(("grp", "ep", "dp"), None),
        P(("grp", "ep", "dp"), None),
        P(("grp", "ep", "dp"), None),
        P(),
        P("ep", None, "dp"),
        P("ep", None, "dp"),
        P("ep", "dp", None),
    )
    out_specs = P(("grp", "ep", "dp"), None)
    return jax.shard_map(body, mesh=mesh, in_specs=in_specs, out_specs=out_specs, check_vma=False)
```

```python
import functools

import jax
import jax.numpy as jnp
from jax import lax
from jax.experimental import pallas as pl
from jax.experimental.pallas import tpu as pltpu
from jax.sharding import PartitionSpec as P

LANES = 128
MIB = 1 << 20
RING = 2
BLOCKS = 4
LIMIT = 26
VMEM = pl.BlockSpec(memory_space=pltpu.VMEM)
HBM = pl.BlockSpec(memory_space=pltpu.HBM)
ANY = pl.BlockSpec(memory_space=pl.ANY)


def pack_kernel(slot_hbm, tokens_hbm, ids_hbm, weight_hbm, out_ref, slot_ref, ids_ref, weight_ref, sem):
    rows, width = tokens_hbm.shape
    copies = [
        pltpu.make_async_copy(slot_hbm, slot_ref, sem.at[0]),
        pltpu.make_async_copy(ids_hbm, ids_ref, sem.at[1]),
        pltpu.make_async_copy(weight_hbm, weight_ref, sem.at[2]),
        pltpu.make_async_copy(tokens_hbm, out_ref.at[:, pl.ds(0, width)], sem.at[3]),
    ]
    for copy in copies:
        copy.start()
    for copy in copies[:3]:
        copy.wait()
    experts = slot_ref.shape[0]
    extra = out_ref.shape[1] - width
    lane = lax.broadcasted_iota(jnp.int32, (rows, extra), 1)
    ids = ids_ref[...]
    weight = weight_ref[...]
    by_slot = jnp.zeros((rows, extra), jnp.float32)
    slot = jnp.zeros(ids.shape, jnp.int32)
    for e in range(experts):
        slot = jnp.where(ids == e, slot_ref[e], slot)
    for k in range(ids.shape[1]):
        by_slot = by_slot + jnp.where(lane == slot[:, k : k + 1], weight[:, k : k + 1], 0.0)
    high = by_slot.astype(jnp.bfloat16)
    low = by_slot - high.astype(jnp.float32)
    low = pltpu.roll(low, experts, 1)
    columns = jnp.where(lane < experts, high.astype(jnp.float32), low)
    copies[3].wait()
    out_ref[:, width:] = columns.astype(jnp.bfloat16)


def join_kernel(*refs):
    row = 0
    for piece in refs[:-1]:
        refs[-1][row : row + piece.shape[0], :] = piece[...]
        row += piece.shape[0]


def join_fetch_kernel(parts, units, *refs):
    pieces = refs[:units]
    up_ref, _, out_ref, ring_ref, held_ref, piece_sem, sem = refs[units:]
    ring, depth, _ = ring_ref.shape
    moves = [
        pltpu.make_async_copy(piece, held_ref.at[u], piece_sem.at[u]) for u, piece in enumerate(pieces)
    ]
    copies = [
        pltpu.make_async_copy(
            up_ref.at[step // parts, pl.ds(step % parts * depth, depth)], ring_ref.at[step], sem.at[step]
        )
        for step in range(ring)
    ]
    for copy in moves + copies:
        copy.start()
    rows = held_ref.shape[1]
    for u, move in enumerate(moves):
        move.wait()
        out_ref[u * rows : (u + 1) * rows, :] = held_ref[u]
    for copy in copies:
        copy.wait()


def join(pieces):
    if len(pieces) == 1:
        return pieces[0]
    rows = sum(piece.shape[0] for piece in pieces)
    width = pieces[0].shape[1]
    return pl.pallas_call(
        join_kernel,
        out_shape=jax.ShapeDtypeStruct((rows, width), jnp.bfloat16),
        in_specs=[VMEM] * len(pieces),
        out_specs=VMEM,
        compiler_params=pltpu.CompilerParams(vmem_limit_bytes=2 * MIB + 8 * rows * width),
        name="join",
    )(*pieces)


def join_fetch(pieces, w_up, held, parts, ring):
    rows = sum(piece.shape[0] for piece in pieces)
    width = pieces[0].shape[1]
    _, depth, ff = w_up.shape
    return pl.pallas_call(
        functools.partial(join_fetch_kernel, parts, len(pieces)),
        out_shape=(
            pltpu.VMEM((rows, width), jnp.bfloat16),
            pltpu.VMEM((ring, depth // parts, ff), jnp.bfloat16),
        ),
        in_specs=[ANY] * len(pieces) + [HBM, VMEM],
        out_specs=(VMEM, VMEM),
        scratch_shapes=[
            pltpu.VMEM((len(pieces), *pieces[0].shape), jnp.bfloat16),
            pltpu.SemaphoreType.DMA((len(pieces),)),
            pltpu.SemaphoreType.DMA((ring,)),
        ],
        compiler_params=pltpu.CompilerParams(vmem_limit_bytes=LIMIT * MIB),
        name="fetch",
    )(*pieces, w_up, held)


def expert_kernel(units, parts, chunk, *refs):
    pieces = refs[:units]
    gate_ref, _, up_ref, down_ref = refs[units : units + 4]
    outs = refs[units + 4 : 2 * units + 4]
    ring_ref, x_ref, coef_ref, hidden_ref, block_ref, up_sem, down_sem = refs[2 * units + 4 :]
    slots, width, ff = gate_ref.shape
    experts = coef_ref.shape[2]
    depth = width // parts
    steps = slots * parts
    ring = ring_ref.shape[0]
    chunks = width // chunk
    blocks = block_ref.shape[0]

    def up_copy(step):
        j, p = step // parts, step % parts
        place = lax.rem(step, ring)
        return pltpu.make_async_copy(
            up_ref.at[j, pl.ds(pl.multiple_of(p * depth, depth), depth)], ring_ref.at[place], up_sem.at[place]
        )

    def down_copy(c, j):
        return pltpu.make_async_copy(
            down_ref.at[j, :, pl.ds(c * chunk, chunk)], block_ref.at[c % blocks, j], down_sem.at[c % blocks, j]
        )

    row = 0
    for piece in pieces:
        count = piece.shape[0]
        x_ref[row : row + count, :] = piece[:, :width]
        coef_ref[0, row : row + count, :] = piece[:, width : width + experts].astype(jnp.float32)
        coef_ref[1, row : row + count, :] = piece[:, width + experts : width + 2 * experts].astype(jnp.float32)
        row += count
    lane = lax.broadcasted_iota(jnp.int32, coef_ref.shape[1:], 1)

    def one(j, carry):
        for c in range(blocks):
            down_copy(c, j).start()
        gate = jnp.dot(x_ref[...], gate_ref[j], preferred_element_type=jnp.float32)
        upper = jnp.zeros(gate.shape, jnp.float32)
        for p in range(parts):
            step = j * parts + p

            @pl.when(step >= ring)
            def _():
                up_copy(step).wait()

            upper = upper + jnp.dot(
                x_ref[:, p * depth : (p + 1) * depth],
                ring_ref[lax.rem(step, ring)],
                preferred_element_type=jnp.float32,
            )

            @pl.when(step + ring < steps)
            def _():
                up_copy(step + ring).start()

        own = lane == lax.axis_index("ep") * slots + j
        coef = jnp.sum(jnp.where(own, coef_ref[0] + coef_ref[1], 0.0), axis=1, keepdims=True)
        hidden = gate / (1.0 + jnp.exp(-gate)) * upper * coef
        hidden_ref[:, pl.ds(pl.multiple_of(j * ff, ff), ff)] = hidden.astype(jnp.bfloat16)
        return carry

    lax.fori_loop(0, slots, one, 0)
    for c in range(chunks):
        for j in range(slots):
            down_copy(c, j).wait()
        block = block_ref[c % blocks].reshape(slots * ff, chunk)
        total = jnp.dot(hidden_ref[...], block, preferred_element_type=jnp.float32).astype(jnp.bfloat16)
        if c + blocks < chunks:
            for j in range(slots):
                down_copy(c + blocks, j).start()
        row = 0
        for out in outs:
            count = out.shape[0]
            out[:, c * chunk : (c + 1) * chunk] = total[row : row + count]
            row += count


def add_kernel(starts, *refs):
    count = refs[-1].shape[0]
    total = None
    for start, ref in zip(starts, refs[:-1]):
        term = ref[start : start + count, :].astype(jnp.float32)
        total = term if total is None else total + term
    refs[-1][...] = total.astype(jnp.bfloat16)


def add(terms, count):
    width = terms[0][0].shape[1]
    return pl.pallas_call(
        functools.partial(add_kernel, [start for _, start in terms]),
        out_shape=jax.ShapeDtypeStruct((count, width), jnp.bfloat16),
        in_specs=[VMEM] * len(terms),
        out_specs=VMEM,
        compiler_params=pltpu.CompilerParams(vmem_limit_bytes=2 * MIB + 32 * count * width),
        name="add",
    )(*[value for value, _ in terms])


def in_vmem(value):
    return pltpu.with_memory_space_constraint(value, pltpu.VMEM)


def toward(size, shift):
    return [(i, (i + shift) % size) for i in range(size)]


def body(tokens, expert_ids, combine_weight, slot_of_expert, w_gate, w_up, w_down):
    ep, dp = lax.axis_size("ep"), lax.axis_size("dp")
    core = 2 if dp % 2 == 0 else 1
    chips = dp // core
    rows, width = tokens.shape
    slots, _, ff = w_gate.shape
    experts = slot_of_expert.shape[0]
    extra = -(-2 * experts // LANES) * LANES
    total_rows = rows * ep * dp
    groups = min(ep, 4)

    def step_z(value, shift):
        return lax.ppermute(value, "ep", toward(ep, shift))

    def step_x(value, shift):
        return lax.ppermute(value, "dp", toward(dp, shift * core))

    def step_core(value):
        return lax.ppermute(value, "dp", [(i, i ^ 1) for i in range(dp)])

    packed = pl.pallas_call(
        pack_kernel,
        out_shape=jax.ShapeDtypeStruct((rows, width + extra), jnp.bfloat16),
        in_specs=[HBM] * 4,
        out_specs=VMEM,
        scratch_shapes=[
            pltpu.SMEM(slot_of_expert.shape, jnp.int32),
            pltpu.VMEM(expert_ids.shape, jnp.int32),
            pltpu.VMEM(combine_weight.shape, jnp.float32),
            pltpu.SemaphoreType.DMA((4,)),
        ],
        cost_estimate=pl.CostEstimate(flops=30 * slots * ff * width * 64, bytes_accessed=64 * MIB, transcendentals=0),
        compiler_params=pltpu.CompilerParams(vmem_limit_bytes=2 * MIB),
        name="pack",
    )(*[pltpu.with_memory_space_constraint(value, pltpu.HBM) for value in (slot_of_expert, tokens, expert_ids, combine_weight)])

    along_z = [packed] + [step_z(packed, -s) for s in range(1, ep)]
    per = ep // groups
    along_z = [join(along_z[g * per : (g + 1) * per]) for g in range(groups)]
    along_x = [[step_x(piece, -s) for piece in along_z] for s in range(1, chips)]
    parts = 2 if width % 256 == 0 else 1
    ring = min(RING, slots * parts)
    gate_in = in_vmem(w_gate)
    joined, fetched = join_fetch(along_z, w_up, gate_in, parts, ring)
    units = [joined] + [join(pieces) for pieces in along_x]
    if core == 2:
        units += [step_core(unit) for unit in units]
    count = len(units)
    unit_rows = ep * rows

    chunk = next(c for c in (1024, 512, 256, 128, width) if width % c == 0)
    blocks = min(BLOCKS, width // chunk)
    *outs, _ = pl.pallas_call(
        functools.partial(expert_kernel, count, parts, chunk),
        out_shape=[pltpu.VMEM((unit_rows, width), jnp.bfloat16)] * count
        + [pltpu.VMEM((ring, width // parts, ff), jnp.bfloat16)],
        in_specs=[VMEM] * (count + 2) + [HBM, HBM],
        out_specs=[VMEM] * (count + 1),
        input_output_aliases={count + 1: count},
        scratch_shapes=[
            pltpu.VMEM((total_rows, width), jnp.bfloat16),
            pltpu.VMEM((2, total_rows, experts), jnp.float32),
            pltpu.VMEM((total_rows, slots * ff), jnp.bfloat16),
            pltpu.VMEM((blocks, slots, ff, chunk), jnp.bfloat16),
            pltpu.SemaphoreType.DMA((ring,)),
            pltpu.SemaphoreType.DMA((blocks, slots)),
        ],
        cost_estimate=pl.CostEstimate(
            flops=6 * total_rows * slots * ff * width,
            bytes_accessed=6 * slots * ff * width,
            transcendentals=total_rows * slots * ff,
        ),
        compiler_params=pltpu.CompilerParams(vmem_limit_bytes=LIMIT * MIB),
        name="expert",
    )(*[in_vmem(value) for value in units], gate_in, in_vmem(fetched), w_up, w_down)

    near, far = outs[:chips], outs[chips:]
    moved = [None] * chips
    if core == 2:
        for s in list(range(1, chips)) + [0]:
            moved[s] = step_core(far[s])

    def here(s, row):
        return [(value[s], row) for value in (near, moved) if value[s] is not None]

    size = per * rows
    order = list(range(1, groups)) + [0]
    arrived = {g: [step_x(add(here(s, g * size), size), s) for s in range(1, chips)] for g in order}

    def piece(s):
        g, row = s // per, s % per * rows
        return here(0, s * rows) + [(value, row) for value in arrived[g]]

    returned = [(step_z(add(piece(s), rows), s), 0) for s in range(1, ep)]
    return add(piece(0) + returned, rows)


def solution(mesh):
    in_specs = (
        P(("grp", "ep", "dp"), None),
        P(("grp", "ep", "dp"), None),
        P(("grp", "ep", "dp"), None),
        P(),
        P("ep", None, "dp"),
        P("ep", None, "dp"),
        P("ep", "dp", None),
    )
    out_specs = P(("grp", "ep", "dp"), None)
    return jax.shard_map(body, mesh=mesh, in_specs=in_specs, out_specs=out_specs, check_vma=False)
```
